512 devices in a mesh: space: 64 (over y, z), orb: 8 (over x, core).
Axes of the slice: x: 4, y: 8, z: 8, core: 2. Of those that a mesh axis runs over, the one named last changes fastest.
Arguments:
- hamiltonian: bfloat16 [512, 7, 256, 256], P('space'), may hold values from -0.125 to 0.125
- orbitals: bfloat16 [256, 131072], P('orb', 'space'), may hold values from -6 to 6
- adjacency: int32 [512, 6], P('space'), may hold values from 0 to 511, as said below
Outputs:
- basis: float32 [256, 131072], P('orb', 'space')
- factor: float32 [256, 256], replicated
The draws below stay inside these ranges and needn't reach their ends.
Inputs may be any that keep to these rules, and one draw needn't show every extreme that they name: `adjacency`: with elements in blocks of 8 (block b holds elements b * 8 to b * 8 + 7), face 0 of an element in block b lies in block b - 1 and face 1 in block b + 1 (both modulo the number of blocks), faces 2 to 5 in block b; for each face, the elements of a block name every element of the target block exactly once.
All inputs are finite; a program needn't handle non-finite values.
Results may differ from the reference program's by a relative error of at most 0.0041.
Values may be sent and summed in bfloat16 or wider, within the bound.
A program may use at most 64 MiB of HBM per device.

```python
import jax
import jax.numpy as jnp
from jax import lax

NB = 256
NORB = 256
ELEM_DEV = 8
ELEMENTS = 512
ROWS = 131072


def draw_adjacency(key, part):
    groups = ELEMENTS // ELEM_DEV
    keys = jax.random.split(jax.random.fold_in(key, 17), groups * 6)
    perms = jax.vmap(lambda k: jax.random.permutation(k, ELEM_DEV))(keys).reshape(groups, 6, ELEM_DEV)
    owner = jnp.arange(groups, dtype=jnp.int32)[:, None]
    offset = jnp.array([-1, 1, 0, 0, 0, 0], dtype=jnp.int32)
    target = (owner + offset[None, :]) % groups
    ident = target[:, :, None] * ELEM_DEV + perms.astype(jnp.int32)
    return ident.transpose(0, 2, 1).reshape(ELEMENTS, 6).astype(jnp.int32)


def shard_levels(stream_key, extent, pieces, least, high):
    level = 1.0
    for position, parts in pieces:
        draws = jax.random.uniform(jax.random.fold_in(jax.random.fold_in(stream_key, 6), position), (parts,), jnp.float32, least / len(pieces), high / len(pieces))
        level = level * jnp.repeat(jnp.exp(draws), extent[position] // parts).reshape((-1,) + (1,) * (len(extent) - 1 - position))
    return level


def bell_draw(rng, extent, width, most, pieces=(), kind=jnp.bfloat16):
    entries = width * jax.random.normal(rng, extent, jnp.float32)
    if pieces:
        entries = entries * shard_levels(rng, extent, pieces, -0.22, 0.18)
    return jnp.clip(entries, -most, most).astype(kind)


def setup_inputs(seed: int = 0) -> dict:
    arg_keys = jax.random.split(jax.random.key(seed), 4)
    return {
        "hamiltonian": bell_draw(arg_keys[0], (ELEMENTS, 7, NB, NB), (7 * NB) ** -0.5, 0.125, ((0, 64),)),
        "orbitals": bell_draw(arg_keys[1], (NORB, ROWS), 1.0, 6.0, ((0, 8), (1, 64))),
        "adjacency": draw_adjacency(jax.random.fold_in(arg_keys[3], 71), 0),
    }


centre = 0.25
radius = 0.75

def apply_ham(hamiltonian, adjacency, vec):
    blocks = vec.reshape(NORB, ELEMENTS, NB).astype(jnp.float32)
    result = jnp.einsum('oej,eij->oei', blocks, hamiltonian[:, 0].astype(jnp.float32))
    for face in range(6):
        near = jnp.take(blocks, adjacency[:, face], axis=1)
        result = result + jnp.einsum('oej,eij->oei', near, hamiltonian[:, face + 1].astype(jnp.float32))
    return result.reshape(NORB, ROWS)

def reference(hamiltonian, orbitals, adjacency):
    level_zero = orbitals.astype(jnp.float32)
    level_one = ((apply_ham(hamiltonian, adjacency, orbitals) - centre * level_zero) / radius).astype(jnp.bfloat16)
    one_wide = level_one.astype(jnp.float32)
    level_two = (2.0 * (apply_ham(hamiltonian, adjacency, level_one) - centre * one_wide) / radius - level_zero).astype(jnp.bfloat16)
    two_wide = level_two.astype(jnp.float32)
    filtered = 2.0 * (apply_ham(hamiltonian, adjacency, level_two) - centre * two_wide) / radius - one_wide
    gram = jnp.dot(filtered, filtered.T, precision=lax.Precision.HIGHEST)
    lower = jnp.linalg.cholesky(gram)
    basis = lax.linalg.triangular_solve(lower, filtered, left_side=True, lower=True)
    return (basis, lower.T)
```

```python
import functools

import jax
import jax.numpy as jnp
from jax import lax
from jax.experimental import pallas as pl
from jax.experimental.pallas import tpu as pltpu
from jax.sharding import PartitionSpec as P

MESH = pl.DeviceIdType.MESH
CENTRE = 0.25
RADIUS = 0.75
F32, BF16 = jnp.float32, jnp.bfloat16
NT = (((1,), (1,)), ((), ()))
DMA = pltpu.SemaphoreType.DMA


def remote(src, dst, send, recv, **where):
    return pltpu.make_async_remote_copy(
        src_ref=src, dst_ref=dst, send_sem=send, recv_sem=recv, device_id=where, device_id_type=MESH
    )


def loop(n, body):
    lax.fori_loop(0, n, lambda i, c: (body(i), c)[1], 0)


def filter_kernel(
    ham_hbm, orb_ref, adj_ref, gram_out, filt_out, low_out,
    ham, lev0, lev1, lev2, lo0, hi0, lo1, hi1, lo2, hi2, part, low, filt, slab, zbuf, ybuf, gram,
    ham_sem, halo_send, halo_recv, ag_send, ag_recv, gg_send, gg_recv,
    red_send, red_recv, out_sem,
):
    level, halo = (lev0, lev1, lev2), ((lo0, hi0), (lo1, hi1), (lo2, hi2))
    space, orb = lax.axis_index("space"), lax.axis_index("orb")
    y, z = space // 8, space % 8
    chip, core = orb // 2, orb % 2
    after, before = (space + 1) % 64, (space + 63) % 64
    partner = chip * 2 + 1 - core
    right = ((chip + 1) % 4) * 2 + core
    left = ((chip + 3) % 4) * 2 + core
    cross = ((chip + 2) % 4) * 2 + core

    def load_ham(e):
        return pltpu.make_async_copy(ham_hbm.at[e], ham.at[e], ham_sem.at[e])

    loop(8, lambda e: load_ham(e).start())

    bar = pltpu.get_barrier_semaphore()
    for where in ({"space": after}, {"space": before}, {"orb": partner}, {"orb": right}, {"orb": left}):
        pl.semaphore_signal(bar, inc=1, device_id=where, device_id_type=MESH)
    for d in range(1, 8):
        pl.semaphore_signal(bar, inc=1, device_id={"space": y * 8 + (z + d) % 8}, device_id_type=MESH)
        pl.semaphore_signal(bar, inc=1, device_id={"space": ((y + d) % 8) * 8 + z}, device_id_type=MESH)
    pl.semaphore_wait(bar, 19)

    def halo_copy(n, side, e):
        src = orb_ref.at[:, pl.ds(pl.multiple_of(e * 256, 256), 256)] if n == 0 else level[n].at[e]
        return remote(src, halo[n][side].at[e], halo_send.at[n, side, e], halo_recv.at[n, side, e],
                      space=after if side == 0 else before)

    def start0(e):
        halo_copy(0, 0, e).start()
        halo_copy(0, 1, e).start()

    loop(8, start0)
    for e in range(8):
        level[0][e] = orb_ref[:, e * 256:(e + 1) * 256]

    def ag_copy(buf, n, send, recv, kind, t):
        if kind == 6:
            raise ValueError
        who = (orb, orb, orb, left, right, cross)[kind]
        dst = (partner, right, left, partner, partner, partner)[kind]
        slot = (0, 1, 2, 4, 5, 6)[kind]
        return remote(buf.at[t, who], buf.at[t, who], send.at[kind, t], recv.at[slot, t], orb=dst)

    def forward(buf, send, recv, t, to_right):
        who = left if to_right else right
        return remote(buf.at[t, who], buf.at[t, who], send.at[6, t], recv.at[3, t],
                      orb=right if to_right else left)

    def arrived(buf, send, recv, slot, t):
        who = (partner, left, right, cross, 0, 0, 0)[slot]
        remote(buf.at[t, who], buf.at[t, who], send.at[0, t], recv.at[slot, t], orb=partner).wait_recv()

    def ag_start(buf, n, send, recv, t):
        for kind in (1, 2, 0):
            ag_copy(buf, n, send, recv, kind, t).start()

    def ag_relay(buf, n, send, recv):
        def near(t, to_right):
            arrived(buf, send, recv, 1, t)
            if to_right:
                forward(buf, send, recv, t, True).start()
            ag_copy(buf, n, send, recv, 3, t).start()
            arrived(buf, send, recv, 2, t)
            if not to_right:
                forward(buf, send, recv, t, False).start()
            ag_copy(buf, n, send, recv, 4, t).start()

        def far(t):
            arrived(buf, send, recv, 3, t)
            ag_copy(buf, n, send, recv, 5, t).start()

        h = n // 2
        loop(h, lambda t: near(t, True))
        loop(n - h, lambda t: near(t + h, False))
        loop(n, far)

    def ag_rest(buf, send, recv, t):
        for slot in (0, 4, 5, 6):
            arrived(buf, send, recv, slot, t)

    def ag_drain(buf, n, send, recv):
        def body(t):
            for kind in range(6):
                ag_copy(buf, n, send, recv, kind, t).wait_send()
            forward(buf, send, recv, t, True).wait_send()
        loop(n, body)

    def dot(v, h):
        return lax.dot_general(v, h, NT, preferred_element_type=F32)

    for n in range(3):
        def inner(e, n=n):
            if n == 0:
                load_ham(e).wait()
            total = dot(level[n][e], ham[e, 0])
            for f in range(2, 6):
                total = total + dot(level[n][adj_ref[e, f] & 7], ham[e, f + 1])
            part[e] = total

        loop(8, inner)

        def landed(e, n=n):
            halo_copy(n, 0, e).wait_recv()
            halo_copy(n, 1, e).wait_recv()

        loop(8, landed)

        def outer(e, n=n):
            total = part[e] + dot(halo[n][0][adj_ref[e, 0] & 7], ham[e, 1])
            total = total + dot(halo[n][1][adj_ref[e, 1] & 7], ham[e, 2])
            total = (total - CENTRE * level[n][e].astype(F32)) * (1.0 / RADIUS)
            if n > 0:
                total = 2.0 * total - level[n - 1][e].astype(F32)
            if n < 2:
                level[n + 1][e] = total.astype(BF16)
                halo_copy(n + 1, 0, e).start()
                halo_copy(n + 1, 1, e).start()
            else:
                high = total.astype(BF16)
                filt[e, orb] = high
                low[e] = (total - high.astype(F32)).astype(BF16)
                ag_start(filt, 8, ag_send, ag_recv, e)

        loop(8, outer)

    ag_relay(filt, 8, ag_send, ag_recv)
    slab[...] = jnp.zeros_like(slab)

    def product(e):
        ag_rest(filt, ag_send, ag_recv, e)
        slab[...] += dot(filt[e, orb], filt[e].reshape(256, 256))

    loop(8, product)
    out_f = pltpu.make_async_copy(filt, filt_out, out_sem.at[0])
    out_f.start()
    out_l = pltpu.make_async_copy(low, low_out, out_sem.at[1])
    out_l.start()

    def red(stage, half, d):
        buf = zbuf if stage == half else ybuf
        mine = z if stage == half else y
        where = y * 8 + (z + d) % 8 if stage == half else ((y + d) % 8) * 8 + z
        return remote(buf.at[half, mine], buf.at[half, mine],
                      red_send.at[stage, half, d], red_recv.at[stage, half, d], space=where)

    order = (4, 3, 5, 2, 6, 1, 7)
    for stage in range(2):
        for half in range(2):
            buf = zbuf if stage == half else ybuf
            mine = z if stage == half else y
            if stage == 0:
                buf[half, mine] = slab[16 * half:16 * half + 16]
            else:
                prev = ybuf if stage == half else zbuf
                for d in order:
                    red(0, half, d).wait_recv()
                total = prev[half, 0]
                for i in range(1, 8):
                    total = total + prev[half, i]
                buf[half, mine] = total
            for d in order:
                red(stage, half, d).start()
    for half in range(2):
        prev = ybuf if half == 0 else zbuf
        for d in order:
            red(1, half, d).wait_recv()
        total = prev[half, 0]
        for i in range(1, 8):
            total = total + prev[half, i]
        gram[half, orb] = total
        ag_start(gram, 2, gg_send, gg_recv, half)
    ag_relay(gram, 2, gg_send, gg_recv)
    loop(2, lambda t: ag_rest(gram, gg_send, gg_recv, t))
    out_g = pltpu.make_async_copy(gram, gram_out, out_sem.at[2])
    out_g.start()

    for n in range(3):
        def sent(e, n=n):
            halo_copy(n, 0, e).wait_send()
            halo_copy(n, 1, e).wait_send()
        loop(8, sent)
    ag_drain(filt, 8, ag_send, ag_recv)
    for stage in range(2):
        for half in range(2):
            for d in order:
                red(stage, half, d).wait_send()
    ag_drain(gram, 2, gg_send, gg_recv)
    out_f.wait()
    out_l.wait()
    out_g.wait()


def filter_call(hamiltonian, orbitals, adjacency):
    anywhere = pl.BlockSpec(memory_space=pl.ANY)
    return pl.pallas_call(
        filter_kernel,
        out_shape=(
            jax.ShapeDtypeStruct((2, 8, 16, 256), F32),
            jax.ShapeDtypeStruct((8, 8, 32, 256), BF16),
            jax.ShapeDtypeStruct((8, 32, 256), BF16),
        ),
        in_specs=[anywhere, pl.BlockSpec(memory_space=pltpu.VMEM), pl.BlockSpec(memory_space=pltpu.SMEM)],
        out_specs=(anywhere, anywhere, anywhere),
        scratch_shapes=[
            pltpu.VMEM((8, 7, 256, 256), BF16),
            *[pltpu.VMEM((8, 32, 256), BF16)] * 9,
            pltpu.VMEM((8, 32, 256), F32),
            pltpu.VMEM((8, 32, 256), BF16),
            pltpu.VMEM((8, 8, 32, 256), BF16),
            pltpu.VMEM((32, 256), F32),
            pltpu.VMEM((2, 8, 16, 256), F32),
            pltpu.VMEM((2, 8, 16, 256), F32),
            pltpu.VMEM((2, 8, 16, 256), F32),
            DMA((8,)),
            DMA((3, 2, 8)), DMA((3, 2, 8)),
            DMA((7, 8)), DMA((7, 8)),
            DMA((7, 2)), DMA((7, 2)),
            DMA((2, 2, 8)), DMA((2, 2, 8)),
            DMA((3,)),
        ],
        compiler_params=pltpu.CompilerParams(
            collective_id=0, has_side_effects=True, vmem_limit_bytes=40 * 2**20
        ),
        name="filter",
    )(hamiltonian, orbitals, adjacency)


def shards(hamiltonian, orbitals, adjacency):
    gram, filt, low = filter_call(hamiltonian, orbitals, adjacency)
    gram = gram.transpose(1, 0, 2, 3).reshape(256, 256)
    lower = jnp.linalg.cholesky(gram)
    inverse = lax.linalg.triangular_solve(lower, jnp.eye(256, dtype=F32), left_side=True, lower=True)
    orb = lax.axis_index("orb")
    rows = lax.dynamic_slice_in_dim(inverse, orb * 32, 32, 0)
    mine = lax.dynamic_slice_in_dim(rows, orb * 32, 32, 1)
    whole = filt.astype(F32).reshape(8, 256, 256)
    basis = jnp.einsum("ro,eoc->rec", rows, whole, precision=lax.Precision.HIGHEST)
    basis = basis + jnp.einsum("ro,eoc->rec", mine, low.astype(F32), precision=lax.Precision.HIGHEST)
    return basis.reshape(32, 2048), lower.T


def solution(mesh):
    in_specs = (P("space", None, None, None), P("orb", "space"), P("space", None))
    out_specs = (P("orb", "space"), P())
    return jax.shard_map(shards, mesh=mesh, in_specs=in_specs, out_specs=out_specs, check_vma=False)
```

```python
import functools

import jax
import jax.numpy as jnp
from jax import lax
from jax.experimental import pallas as pl
from jax.experimental.pallas import tpu as pltpu
from jax.sharding import PartitionSpec as P

MESH = pl.DeviceIdType.MESH
CENTRE = 0.25
RADIUS = 0.75
F32, BF16 = jnp.float32, jnp.bfloat16
NT = (((1,), (1,)), ((), ()))
DMA = pltpu.SemaphoreType.DMA


def remote(src, dst, send, recv, **where):
    return pltpu.make_async_remote_copy(
        src_ref=src, dst_ref=dst, send_sem=send, recv_sem=recv, device_id=where, device_id_type=MESH
    )


def loop(n, body):
    lax.fori_loop(0, n, lambda i, c: (body(i), c)[1], 0)


def filter_kernel(
    ham_hbm, orb_hbm, adj_hbm, gram_a_out, gram_b_out, filt_out, low_out,
    ham, adj, lev0, lev1, lev2, lo0, hi0, lo1, hi1, lo2, hi2, part, low, filt, near_sum, far_sum,
    za, ya, yb, zb, gram_a, gram_b,
    ham_sem, in_sem, token, halo_send, halo_recv, ag_send, ag_recv, gg_send, gg_recv,
    red_send, red_recv, out_sem,
):
    level, halo = (lev0, lev1, lev2), ((lo0, hi0), (lo1, hi1), (lo2, hi2))
    space, orb = lax.axis_index("space"), lax.axis_index("orb")
    y, z = space // 8, space % 8
    chip, core = orb // 2, orb % 2
    after, before = (space + 1) % 64, (space + 63) % 64
    chip_r, chip_l, chip_x = (chip + 1) % 4, (chip + 3) % 4, (chip + 2) % 4
    partner = chip * 2 + 1 - core
    right, left = chip_r * 2 + core, chip_l * 2 + core
    left_to = chip_l * 2 + (core + chip_l // 2) % 2
    from_l = left
    from_r = chip_r * 2 + (core + chip // 2) % 2
    from_x = chip_x * 2 + core
    from_y = chip_x * 2 + (core + chip_r // 2) % 2
    pair = chip * 2 + (core + 1 + chip // 2) % 2

    def load_ham(e):
        return pltpu.make_async_copy(ham_hbm.at[e], ham.at[e], ham_sem.at[e])

    def load_level(e):
        src = orb_hbm.at[:, pl.ds(pl.multiple_of(e * 256, 256), 256)]
        return pltpu.make_async_copy(src, lev0.at[e], in_sem.at[e])

    load_adj = pltpu.make_async_copy(adj_hbm, adj, in_sem.at[8])

    close = (
        {"space": after}, {"space": before},
        {"space": y * 8 + (z + 1) % 8}, {"space": y * 8 + (z + 7) % 8},
        {"space": (y + 1) % 8 * 8 + z}, {"space": (y + 7) % 8 * 8 + z},
        {"orb": partner}, {"orb": chip_r * 2}, {"orb": chip_r * 2 + 1}, {"orb": chip_l * 2}, {"orb": chip_l * 2 + 1},
    )
    bar = pltpu.get_barrier_semaphore()
    for where in close:
        pl.semaphore_signal(bar, inc=1, device_id=where, device_id_type=MESH)
    load_adj.start()
    loop(8, lambda e: load_level(e).start())
    loop(8, lambda e: load_ham(e).start())
    pl.semaphore_wait(bar, len(close))

    def halo_copy(n, side, e):
        src = orb_hbm.at[:, pl.ds(pl.multiple_of(e * 256, 256), 256)] if n == 0 else level[n].at[e]
        return remote(src, halo[n][side].at[e], halo_send.at[n, side, e], halo_recv.at[n, side, e],
                      space=after if side == 0 else before)

    def start0(e):
        halo_copy(0, 0, e).start()
        halo_copy(0, 1, e).start()

    loop(8, start0)

    def pass_token(n):
        for where in close:
            pl.semaphore_signal(token.at[n], inc=1, device_id=where, device_id_type=MESH)

    def take_token(n):
        pl.semaphore_wait(token.at[n], len(close))

    pass_token(0)

    def gather(kind, t):
        who = (orb, orb, orb, from_l, from_r, from_x, from_l, from_r, from_y)[kind]
        dst = (right, left_to, partner, partner, partner, partner, right, left, partner)[kind]
        send = (0, 1, 2, 3, 4, 5, 6, 6, 5)[kind]
        slot = (0, 1, 2, 3, 4, 5, 6, 6, 5)[kind]
        return remote(filt.at[t, who], filt.at[t, who], ag_send.at[send, t], ag_recv.at[slot, t], orb=dst)

    def arrived(slot, t):
        remote(filt.at[t, orb], filt.at[t, orb], ag_send.at[0, t], ag_recv.at[slot, t], orb=partner).wait_recv()

    def dot(v, h):
        return lax.dot_general(v, h, NT, preferred_element_type=F32)

    load_adj.wait()
    loop(8, lambda e: load_level(e).wait())
    for n in range(3):
        def inner(e, n=n):
            if n == 0:
                load_ham(e).wait()
            total = dot(level[n][e], ham[e, 0])
            for f in range(2, 6):
                total = total + dot(level[n][adj[e, f] & 7], ham[e, f + 1])
            part[e] = total

        loop(8, inner)
        take_token(n)
        if n < 2:
            pass_token(n + 1)

        def landed(e, n=n):
            halo_copy(n, 0, e).wait_recv()
            halo_copy(n, 1, e).wait_recv()

        loop(8, landed)

        def outer(e, n=n):
            total = part[e] + dot(halo[n][0][adj[e, 0] & 7], ham[e, 1])
            total = total + dot(halo[n][1][adj[e, 1] & 7], ham[e, 2])
            total = (total - CENTRE * level[n][e].astype(F32)) * (1.0 / RADIUS)
            if n > 0:
                total = 2.0 * total - level[n - 1][e].astype(F32)
            if n < 2:
                level[n + 1][e] = total.astype(BF16)
                halo_copy(n + 1, 0, e).start()
                halo_copy(n + 1, 1, e).start()
            else:
                high = total.astype(BF16)
                filt[e, orb] = high
                low[e] = (total - high.astype(F32)).astype(BF16)
                for kind in range(3):
                    gather(kind, e).start()

        loop(8, outer)

    near_sum[...] = jnp.zeros_like(near_sum)
    far_sum[...] = jnp.zeros_like(far_sum)

    def product(t, first):
        arrived(0, t)
        if first:
            gather(6, t).start()
        gather(3, t).start()
        arrived(1, t)
        if not first:
            gather(7, t).start()
        gather(4, t).start()
        arrived(2, t)
        mine, west = filt[t, orb], filt[t, from_l]
        near_sum[...] += dot(mine, jnp.concatenate([mine, filt[t, partner], west, mine], axis=0))
        far_sum[...] += dot(filt[t, from_r], jnp.concatenate([west, west, west, filt[t, pair]], axis=0))

    loop(4, lambda t: product(t, True))
    loop(4, lambda t: product(t + 4, False))

    order = (4, 3, 5, 2, 6, 1, 7)
    bufs = ((za, ya), (yb, zb))

    def red(stage, half, d):
        along_z = stage == half
        buf = bufs[half][stage]
        mine = z if along_z else y
        where = y * 8 + (z + d) % 8 if along_z else ((y + d) % 8) * 8 + z
        return remote(buf.at[mine], buf.at[mine],
                      red_send.at[stage, half, d], red_recv.at[stage, half, d], space=where)

    def summed(stage, half):
        buf = bufs[half][stage]
        for d in order:
            red(stage, half, d).wait_recv()
        total = buf[0]
        for i in range(1, 8):
            total = total + buf[i]
        return total

    lane = lax.broadcasted_iota(jnp.int32, (32, 128), 1)
    main = jnp.where(lane < 96, near_sum[...], far_sum[...])
    lane8 = lax.broadcasted_iota(jnp.int32, (8, 128), 1)
    fold = far_sum[0:8]
    fold = jnp.where(lane8 < 32, fold, far_sum[8:16])
    fold = jnp.where(lane8 < 64, fold, far_sum[16:24])
    rest = jnp.where(lane8 < 96, fold, pltpu.roll(far_sum[24:32], 96, 1))
    za[z] = main[:24]
    yb[y, 0:8] = main[24:]
    yb[y, 8:16] = rest
    for half in range(2):
        for d in order:
            red(0, half, d).start()
    for half in range(2):
        total = summed(0, half)
        if half == 0:
            ya[y] = total
        else:
            zb[z] = total
        for d in order:
            red(1, half, d).start()

    def across_first(t):
        arrived(6, t)
        gather(5, t).start()

    def across_second(t):
        arrived(6, t + 4)
        gather(8, t + 4).start()

    loop(4, across_first)
    loop(4, across_second)

    def share(half, d):
        buf = gram_b if half else gram_a
        return remote(buf.at[orb], buf.at[orb], gg_send.at[half, d], gg_recv.at[half, d], orb=(orb + d) % 8)

    for half in range(2):
        total = summed(1, half)
        (gram_b if half else gram_a)[orb] = total
        for d in order:
            share(half, d).start()

    def rest_landed(t):
        for slot in (3, 4, 5):
            arrived(slot, t)

    loop(8, rest_landed)
    out_f = pltpu.make_async_copy(filt, filt_out, out_sem.at[0])
    out_f.start()
    out_l = pltpu.make_async_copy(low, low_out, out_sem.at[1])
    out_l.start()
    for n in range(3):
        def sent(e, n=n):
            halo_copy(n, 0, e).wait_send()
            halo_copy(n, 1, e).wait_send()
        loop(8, sent)

    def gathered(t):
        for kind in range(7):
            gather(kind, t).wait_send()

    loop(8, gathered)
    for stage in range(2):
        for half in range(2):
            for d in order:
                red(stage, half, d).wait_send()
    for half in range(2):
        for d in order:
            share(half, d).wait_recv()
    out_a = pltpu.make_async_copy(gram_a, gram_a_out, out_sem.at[2])
    out_a.start()
    out_b = pltpu.make_async_copy(gram_b, gram_b_out, out_sem.at[3])
    out_b.start()
    for half in range(2):
        for d in order:
            share(half, d).wait_send()
    for out in (out_f, out_l, out_a, out_b):
        out.wait()


def filter_call(hamiltonian, orbitals, adjacency):
    anywhere = pl.BlockSpec(memory_space=pl.ANY)
    outside = pl.BlockSpec(memory_space=pltpu.HBM)
    return pl.pallas_call(
        filter_kernel,
        out_shape=(
            jax.ShapeDtypeStruct((8, 24, 128), F32),
            jax.ShapeDtypeStruct((8, 16, 128), F32),
            jax.ShapeDtypeStruct((8, 8, 32, 256), BF16),
            jax.ShapeDtypeStruct((8, 32, 256), BF16),
        ),
        in_specs=[outside, outside, outside],
        out_specs=(anywhere,) * 4,
        scratch_shapes=[
            pltpu.VMEM((8, 7, 256, 256), BF16),
            pltpu.SMEM((8, 6), jnp.int32),
            *[pltpu.VMEM((8, 32, 256), BF16)] * 9,
            pltpu.VMEM((8, 32, 256), F32),
            pltpu.VMEM((8, 32, 256), BF16),
            pltpu.VMEM((8, 8, 32, 256), BF16),
            pltpu.VMEM((32, 128), F32), pltpu.VMEM((32, 128), F32),
            *[pltpu.VMEM((8, 24, 128), F32)] * 2,
            *[pltpu.VMEM((8, 16, 128), F32)] * 2,
            pltpu.VMEM((8, 24, 128), F32), pltpu.VMEM((8, 16, 128), F32),
            DMA((8,)), DMA((9,)), pltpu.SemaphoreType.REGULAR((3,)),
            DMA((3, 2, 8)), DMA((3, 2, 8)),
            DMA((7, 8)), DMA((7, 8)),
            DMA((2, 8)), DMA((2, 8)),
            DMA((2, 2, 8)), DMA((2, 2, 8)),
            DMA((4,)),
        ],
        compiler_params=pltpu.CompilerParams(
            collective_id=0, has_side_effects=True, vmem_limit_bytes=40 * 2**20
        ),
        name="filter",
    )(hamiltonian, orbitals, adjacency)


TN = (((0,), (0,)), ((), ()))
NN = (((1,), (0,)), ((), ()))


def exact_dot(a, b, dims):
    return lax.dot_general(a, b, dims, precision=lax.Precision.HIGHEST, preferred_element_type=F32)


def spread(x, i, j):
    return jnp.broadcast_to(x[i:i + 1, j:j + 1], (8, 128))


def factor_block(tiles):
    sub = lax.broadcasted_iota(jnp.int32, (8, 128), 0)
    tiles = list(tiles)
    done = []
    for s in range(8):
        tile = tiles[s]
        at = [[spread(tile, i, 8 * s + j) if j >= i else None for j in range(8)] for i in range(8)]
        rows = [jnp.broadcast_to(tile[k:k + 1, :], (8, 128)) for k in range(8)]
        cols = {g: [jnp.broadcast_to(tiles[g][:, 8 * s + k:8 * s + k + 1], (8, 128)) for k in range(8)]
                for g in range(s + 1, 8)}
        for k in range(8):
            r = lax.rsqrt(at[k][k])
            r = r * (1.5 - 0.5 * at[k][k] * r * r)
            rows[k] = rows[k] * r
            for j in range(k + 1, 8):
                at[k][j] = at[k][j] * r
            for g in cols:
                cols[g][k] = cols[g][k] * r
            for i in range(k + 1, 8):
                for j in range(i, 8):
                    at[i][j] = at[i][j] - at[k][i] * at[k][j]
                rows[i] = rows[i] - at[k][i] * rows[k]
                for g in cols:
                    cols[g][i] = cols[g][i] - at[k][i] * cols[g][k]
        for g in cols:
            t = tiles[g]
            for k in range(8):
                t = t - cols[g][k] * rows[k]
            tiles[g] = t
        out = rows[0]
        for k in range(1, 8):
            out = jnp.where(sub == k, rows[k], out)
        done.append(out)
    return jnp.concatenate(done, axis=0)


def finish_kernel(gram_a_ref, gram_b_ref, filt_hbm, low_hbm, basis_ref, factor_ref, work, rest, inv, filt, low, sem):
    load_f = pltpu.make_async_copy(filt_hbm, filt, sem.at[0])
    load_f.start()
    load_l = pltpu.make_async_copy(low_hbm, low, sem.at[1])
    load_l.start()
    def place(i, j, block):
        if i // 2 > j // 2:
            i, j, block = j, i, block.T
        work[32 * i:32 * i + 32, 32 * j:32 * j + 32] = block

    for o in range(8):
        chip, core = o // 2, o % 2
        left = (chip + 3) % 4 * 2 + core
        right = (chip + 1) % 4 * 2 + (core + chip // 2) % 2
        pair = chip * 2 + (core + 1 + chip // 2) % 2
        top = jnp.concatenate([gram_a_ref[o], gram_b_ref[o, 0:8]], axis=0)
        fold = gram_b_ref[o, 8:16]
        place(o, o, top[:, :32])
        place(o, o ^ 1, top[:, 32:64])
        place(o, left, top[:, 64:96])
        place(right, pair, top[:, 96:])
        place(right, left, jnp.concatenate([fold[:, 32 * q:32 * q + 32] for q in range(4)], axis=0))
    eye = (lax.broadcasted_iota(jnp.int32, (64, 64), 0) == lax.broadcasted_iota(jnp.int32, (64, 64), 1)).astype(F32)
    upper = lax.broadcasted_iota(jnp.int32, (64, 64), 0) <= lax.broadcasted_iota(jnp.int32, (64, 64), 1)
    lower = lax.broadcasted_iota(jnp.int32, (64, 64), 0) >= lax.broadcasted_iota(jnp.int32, (64, 64), 1)
    rest[...] = jnp.zeros_like(rest)
    inv[...] = jnp.zeros_like(inv)
    factor_ref[...] = jnp.zeros_like(factor_ref)
    for p in range(4):
        a, b = 64 * p, 64 * p + 64
        block = jnp.concatenate([work[a:b, a:b], eye], axis=1)
        solved = factor_block([block[8 * s:8 * s + 8] for s in range(8)])
        factor_ref[a:b, a:b] = jnp.where(upper, solved[:, :64], 0.0)
        own = jnp.where(lower, solved[:, 64:], 0.0)
        inv[a:b, a:b] = own
        if p > 0:
            inv[a:b, :a] = exact_dot(own, rest[a:b, :a], NN)
        if p < 3:
            u = exact_dot(own, work[a:b, b:], NN)
            factor_ref[a:b, b:] = u
            work[b:, b:] = work[b:, b:] - exact_dot(u, u, TN)
            rest[b:, :b] = rest[b:, :b] - exact_dot(u, inv[a:b, :b], TN)
    orb = lax.axis_index("orb")
    mine = inv[pl.ds(pl.multiple_of(orb * 32, 32), 32), :]
    high = mine.astype(BF16)
    left = mine - high.astype(F32)
    mid = left.astype(BF16)
    tail = (left - mid.astype(F32)).astype(BF16)
    stack = jnp.concatenate([high, mid, tail], axis=0)
    here = pltpu.roll(mine, (256 - orb * 32) % 256, 1)[:, :32].astype(BF16)
    load_f.wait()
    load_l.wait()

    for e in range(8):
        d = lax.dot_general(stack, filt[e].reshape(256, 256), NN, preferred_element_type=F32)
        c = lax.dot_general(here, low[e], NN, preferred_element_type=F32)
        basis_ref[:, e * 256:(e + 1) * 256] = d[:32] + (d[32:64] + (d[64:] + c))


def finish_call(gram_a, gram_b, filt, low):
    anywhere = pl.BlockSpec(memory_space=pl.ANY)
    vmem = pl.BlockSpec(memory_space=pltpu.VMEM)
    return pl.pallas_call(
        finish_kernel,
        out_shape=(jax.ShapeDtypeStruct((32, 2048), F32), jax.ShapeDtypeStruct((256, 256), F32)),
        in_specs=[vmem, vmem, anywhere, anywhere],
        out_specs=(vmem, vmem),
        scratch_shapes=[
            pltpu.VMEM((256, 256), F32), pltpu.VMEM((256, 256), F32), pltpu.VMEM((256, 256), F32),
            pltpu.VMEM((8, 8, 32, 256), BF16), pltpu.VMEM((8, 32, 256), BF16), DMA((2,)),
        ],
        compiler_params=pltpu.CompilerParams(vmem_limit_bytes=40 * 2**20),
        name="finish",
    )(gram_a, gram_b, filt, low)


def shards(hamiltonian, orbitals, adjacency):
    return finish_call(*filter_call(hamiltonian, orbitals, adjacency))


def solution(mesh):
    in_specs = (P("space", None, None, None), P("orb", "space"), P("space", None))
    out_specs = (P("orb", "space"), P())
    return jax.shard_map(shards, mesh=mesh, in_specs=in_specs, out_specs=out_specs, check_vma=False)
```

```python
import functools

import jax
import jax.numpy as jnp
from jax import lax
from jax.experimental import pallas as pl
from jax.experimental.pallas import tpu as pltpu
from jax.sharding import PartitionSpec as P

MESH = pl.DeviceIdType.MESH
CENTRE = 0.25
RADIUS = 0.75
F32, BF16 = jnp.float32, jnp.bfloat16
NT = (((1,), (1,)), ((), ()))
DMA = pltpu.SemaphoreType.DMA


def remote(src, dst, send, recv, **where):
    return pltpu.make_async_remote_copy(
        src_ref=src, dst_ref=dst, send_sem=send, recv_sem=recv, device_id=where, device_id_type=MESH
    )


def loop(n, body):
    lax.fori_loop(0, n, lambda i, c: (body(i), c)[1], 0)


def filter_kernel(
    ham_hbm, orb_hbm, adj_hbm, gram_a_out, gram_b_out, filt_out, low_out,
    ham, adj, lev0, lev1, lev2, lo0, hi0, lo1, hi1, lo2, hi2, part, low, filt, near_sum, far_sum,
    za, ya, yb, zb, gram_a, gram_b,
    ham_sem, in_sem, token, halo_send, halo_recv, ag_send, ag_recv, gg_send, gg_recv,
    red_send, red_recv, out_sem,
):
    level, halo = (lev0, lev1, lev2), ((lo0, hi0), (lo1, hi1), (lo2, hi2))
    space, orb = lax.axis_index("space"), lax.axis_index("orb")
    y, z = space // 8, space % 8
    chip, core = orb // 2, orb % 2
    after, before = (space + 1) % 64, (space + 63) % 64
    chip_r, chip_l, chip_x = (chip + 1) % 4, (chip + 3) % 4, (chip + 2) % 4
    partner = chip * 2 + 1 - core
    right, left = chip_r * 2 + core, chip_l * 2 + core
    left_to = chip_l * 2 + (core + chip_l // 2) % 2
    from_l = left
    from_r = chip_r * 2 + (core + chip // 2) % 2
    from_x = chip_x * 2 + core
    from_y = chip_x * 2 + (core + chip_r // 2) % 2
    pair = chip * 2 + (core + 1 + chip // 2) % 2

    def load_ham(e):
        return pltpu.make_async_copy(ham_hbm.at[e], ham.at[e], ham_sem.at[e])

    def load_level(e):
        src = orb_hbm.at[:, pl.ds(pl.multiple_of(e * 256, 256), 256)]
        return pltpu.make_async_copy(src, lev0.at[e], in_sem.at[e])

    load_adj = pltpu.make_async_copy(adj_hbm, adj, in_sem.at[8])

    close = (
        {"space": after}, {"space": before},
        {"space": y * 8 + (z + 1) % 8}, {"space": y * 8 + (z + 7) % 8},
        {"space": (y + 1) % 8 * 8 + z}, {"space": (y + 7) % 8 * 8 + z},
        {"orb": partner}, {"orb": chip_r * 2}, {"orb": chip_r * 2 + 1}, {"orb": chip_l * 2}, {"orb": chip_l * 2 + 1},
    )
    bar = pltpu.get_barrier_semaphore()
    for where in close:
        pl.semaphore_signal(bar, inc=1, device_id=where, device_id_type=MESH)
    load_adj.start()
    loop(8, lambda e: load_level(e).start())
    loop(8, lambda e: load_ham(e).start())
    pl.semaphore_wait(bar, len(close))

    def halo_copy(n, side, e):
        src = orb_hbm.at[:, pl.ds(pl.multiple_of(e * 256, 256), 256)] if n == 0 else level[n].at[e]
        return remote(src, halo[n][side].at[e], halo_send.at[n, side, e], halo_recv.at[n, side, e],
                      space=after if side == 0 else before)

    def start0(e):
        halo_copy(0, 0, e).start()
        halo_copy(0, 1, e).start()

    loop(8, start0)

    def pass_token(n):
        for where in close:
            pl.semaphore_signal(token.at[n], inc=1, device_id=where, device_id_type=MESH)

    def take_token(n):
        pl.semaphore_wait(token.at[n], len(close))

    pass_token(0)

    def gather(kind, t):
        who = (orb, orb, orb, from_l, from_r, from_x, from_l, from_r, from_y)[kind]
        dst = (right, left_to, partner, partner, partner, partner, right, left, partner)[kind]
        send = (0, 1, 2, 3, 4, 5, 6, 6, 5)[kind]
        slot = (0, 1, 2, 3, 4, 5, 6, 6, 5)[kind]
        return remote(filt.at[t, who], filt.at[t, who], ag_send.at[send, t], ag_recv.at[slot, t], orb=dst)

    def arrived(slot, t):
        remote(filt.at[t, orb], filt.at[t, orb], ag_send.at[0, t], ag_recv.at[slot, t], orb=partner).wait_recv()

    def dot(v, h):
        return lax.dot_general(v, h, NT, preferred_element_type=F32)

    load_adj.wait()
    loop(8, lambda e: load_level(e).wait())
    for n in range(3):
        def inner(e, n=n):
            if n == 0:
                load_ham(e).wait()
            total = dot(level[n][e], ham[e, 0])
            for f in range(2, 6):
                total = total + dot(level[n][adj[e, f] & 7], ham[e, f + 1])
            part[e] = total

        loop(8, inner)
        take_token(n)
        if n < 2:
            pass_token(n + 1)

        def landed(e, n=n):
            halo_copy(n, 0, e).wait_recv()
            halo_copy(n, 1, e).wait_recv()

        loop(8, landed)

        def outer(group, n=n):
            ids = [group * 4 + i for i in range(4)]
            totals = []
            for e in ids:
                total = part[e] + dot(halo[n][0][adj[e, 0] & 7], ham[e, 1])
                total = total + dot(halo[n][1][adj[e, 1] & 7], ham[e, 2])
                total = (total - CENTRE * level[n][e].astype(F32)) * (1.0 / RADIUS)
                if n > 0:
                    total = 2.0 * total - level[n - 1][e].astype(F32)
                totals.append(total)
            for e, total in zip(ids, totals):
                if n < 2:
                    level[n + 1][e] = total.astype(BF16)
                else:
                    high = total.astype(BF16)
                    filt[e, orb] = high
                    low[e] = (total - high.astype(F32)).astype(BF16)
            for e in ids:
                if n < 2:
                    halo_copy(n + 1, 0, e).start()
                    halo_copy(n + 1, 1, e).start()
                else:
                    for kind in range(3):
                        gather(kind, e).start()

        loop(2, outer)

    near_sum[...] = jnp.zeros_like(near_sum)
    far_sum[...] = jnp.zeros_like(far_sum)

    def product(half):
        mine, mate, west, east, twin = [], [], [], [], []
        for t in [half * 2 + i for i in range(2)]:
            for slot in range(3):
                arrived(slot, t)
            mine.append(filt[t, orb])
            mate.append(filt[t, partner])
            west.append(filt[t, from_l])
            east.append(filt[t, from_r])
            twin.append(filt[t, pair])
        mine, mate, west, east, twin = (jnp.concatenate(x, axis=1) for x in (mine, mate, west, east, twin))
        near_sum[...] += dot(mine, jnp.concatenate([mine, mate, west, mine], axis=0))
        far_sum[...] += dot(east, jnp.concatenate([west, west, west, twin], axis=0))

    loop(4, product)

    order = (4, 3, 5, 2, 6, 1, 7)
    bufs = ((za, ya), (yb, zb))

    def red(stage, half, d):
        along_z = stage == half
        buf = bufs[half][stage]
        mine = z if along_z else y
        where = y * 8 + (z + d) % 8 if along_z else ((y + d) % 8) * 8 + z
        return remote(buf.at[mine], buf.at[mine],
                      red_send.at[stage, half, d], red_recv.at[stage, half, d], space=where)

    def summed(stage, half):
        buf = bufs[half][stage]
        for d in order:
            red(stage, half, d).wait_recv()
        total = buf[0]
        for i in range(1, 8):
            total = total + buf[i]
        return total

    lane = lax.broadcasted_iota(jnp.int32, (32, 128), 1)
    main = jnp.where(lane < 96, near_sum[...], far_sum[...])
    lane8 = lax.broadcasted_iota(jnp.int32, (8, 128), 1)
    fold = far_sum[0:8]
    fold = jnp.where(lane8 < 32, fold, far_sum[8:16])
    fold = jnp.where(lane8 < 64, fold, far_sum[16:24])
    rest = jnp.where(lane8 < 96, fold, pltpu.roll(far_sum[24:32], 96, 1))
    za[z] = main[:24]
    yb[y, 0:8] = main[24:]
    yb[y, 8:16] = rest
    for half in range(2):
        for d in order:
            red(0, half, d).start()

    def pass_on(t):
        gather(6, t).start()
        gather(7, t + 4).start()

    def relay(t):
        gather(3, t).start()
        gather(4, t).start()

    loop(4, pass_on)
    loop(8, relay)
    for half in range(2):
        total = summed(0, half)
        if half == 0:
            ya[y] = total
        else:
            zb[z] = total
        for d in order:
            red(1, half, d).start()

    def across_first(t):
        arrived(6, t)
        gather(5, t).start()

    def across_second(t):
        arrived(6, t + 4)
        gather(8, t + 4).start()

    loop(4, across_first)
    loop(4, across_second)

    def share(half, d):
        buf = gram_b if half else gram_a
        return remote(buf.at[orb], buf.at[orb], gg_send.at[half, d], gg_recv.at[half, d], orb=(orb + d) % 8)

    for half in range(2):
        total = summed(1, half)
        (gram_b if half else gram_a)[orb] = total
        for d in order:
            share(half, d).start()

    def rest_landed(t):
        for slot in (3, 4, 5):
            arrived(slot, t)

    loop(8, rest_landed)
    out_f = pltpu.make_async_copy(filt, filt_out, out_sem.at[0])
    out_f.start()
    out_l = pltpu.make_async_copy(low, low_out, out_sem.at[1])
    out_l.start()
    for n in range(3):
        def sent(e, n=n):
            halo_copy(n, 0, e).wait_send()
            halo_copy(n, 1, e).wait_send()
        loop(8, sent)

    def gathered(t):
        for kind in range(7):
            gather(kind, t).wait_send()

    loop(8, gathered)
    for stage in range(2):
        for half in range(2):
            for d in order:
                red(stage, half, d).wait_send()
    for half in range(2):
        for d in order:
            share(half, d).wait_recv()
    out_a = pltpu.make_async_copy(gram_a, gram_a_out, out_sem.at[2])
    out_a.start()
    out_b = pltpu.make_async_copy(gram_b, gram_b_out, out_sem.at[3])
    out_b.start()
    for half in range(2):
        for d in order:
            share(half, d).wait_send()
    for out in (out_f, out_l, out_a, out_b):
        out.wait()


def filter_call(hamiltonian, orbitals, adjacency):
    anywhere = pl.BlockSpec(memory_space=pl.ANY)
    outside = pl.BlockSpec(memory_space=pltpu.HBM)
    return pl.pallas_call(
        filter_kernel,
        out_shape=(
            jax.ShapeDtypeStruct((8, 24, 128), F32),
            jax.ShapeDtypeStruct((8, 16, 128), F32),
            jax.ShapeDtypeStruct((8, 8, 32, 256), BF16),
            jax.ShapeDtypeStruct((8, 32, 256), BF16),
        ),
        in_specs=[outside, outside, outside],
        out_specs=(anywhere,) * 4,
        scratch_shapes=[
            pltpu.VMEM((8, 7, 256, 256), BF16),
            pltpu.SMEM((8, 6), jnp.int32),
            *[pltpu.VMEM((8, 32, 256), BF16)] * 9,
            pltpu.VMEM((8, 32, 256), F32),
            pltpu.VMEM((8, 32, 256), BF16),
            pltpu.VMEM((8, 8, 32, 256), BF16),
            pltpu.VMEM((32, 128), F32), pltpu.VMEM((32, 128), F32),
            *[pltpu.VMEM((8, 24, 128), F32)] * 2,
            *[pltpu.VMEM((8, 16, 128), F32)] * 2,
            pltpu.VMEM((8, 24, 128), F32), pltpu.VMEM((8, 16, 128), F32),
            DMA((8,)), DMA((9,)), pltpu.SemaphoreType.REGULAR((3,)),
            DMA((3, 2, 8)), DMA((3, 2, 8)),
            DMA((7, 8)), DMA((7, 8)),
            DMA((2, 8)), DMA((2, 8)),
            DMA((2, 2, 8)), DMA((2, 2, 8)),
            DMA((4,)),
        ],
        compiler_params=pltpu.CompilerParams(
            collective_id=0, has_side_effects=True, vmem_limit_bytes=67043328
        ),
        name="filter",
    )(hamiltonian, orbitals, adjacency)


SIZE = 64
EARLY = False
TN = (((0,), (0,)), ((), ()))
NN = (((1,), (0,)), ((), ()))


def exact_dot(a, b, dims):
    return lax.dot_general(a, b, dims, precision=lax.Precision.HIGHEST, preferred_element_type=F32)


def spread(x, i, j):
    return jnp.broadcast_to(x[i:i + 1, j:j + 1], (8, 128))


def factor_block(tiles):
    n, width = len(tiles), tiles[0].shape[1]
    sub = lax.broadcasted_iota(jnp.int32, (8, width), 0)
    tiles = list(tiles)
    done = []
    for s in range(n):
        tile = tiles[s]
        at = [[spread(tile, i, 8 * s + j) if j >= i else None for j in range(8)] for i in range(8)]
        rows = [jnp.broadcast_to(tile[k:k + 1, :], (8, width)) for k in range(8)]
        cols = {g: [jnp.broadcast_to(tiles[g][:, 8 * s + k:8 * s + k + 1], (8, 128)) for k in range(8)]
                for g in range(s + 1, n)}
        wide = lambda x: jnp.concatenate([x] * (width // 128), axis=1)
        for k in range(8):
            r = lax.rsqrt(at[k][k])
            rows[k] = rows[k] * wide(r)
            for j in range(k + 1, 8):
                at[k][j] = at[k][j] * r
            for g in cols:
                cols[g][k] = cols[g][k] * r
            for i in range(k + 1, 8):
                for j in range(i, 8):
                    at[i][j] = at[i][j] - at[k][i] * at[k][j]
                rows[i] = rows[i] - wide(at[k][i]) * rows[k]
                for g in cols:
                    cols[g][i] = cols[g][i] - at[k][i] * cols[g][k]
        for g in cols:
            t = tiles[g]
            for k in range(8):
                t = t - wide(cols[g][k]) * rows[k]
            tiles[g] = t
        out = rows[0]
        for k in range(1, 8):
            out = jnp.where(sub == k, rows[k], out)
        done.append(out)
    return jnp.concatenate(done, axis=0)


def finish_kernel(
    gram_a_hbm, gram_b_hbm, filt_hbm, low_hbm, basis_ref, factor_ref,
    work, rest, inv, gram_a_ref, gram_b_ref, filt, low, sem,
):
    load_a = pltpu.make_async_copy(gram_a_hbm, gram_a_ref, sem.at[2])
    load_a.start()
    load_b = pltpu.make_async_copy(gram_b_hbm, gram_b_ref, sem.at[3])
    load_b.start()
    load_f = pltpu.make_async_copy(filt_hbm, filt, sem.at[0])
    load_f.start()
    load_l = pltpu.make_async_copy(low_hbm, low, sem.at[1])
    load_l.start()
    rest[...] = jnp.zeros_like(rest)
    inv[...] = jnp.zeros_like(inv)
    factor_ref[...] = jnp.zeros_like(factor_ref)
    load_a.wait()
    load_b.wait()

    def place(i, j, block):
        if 32 * i // SIZE > 32 * j // SIZE:
            i, j, block = j, i, block.T
        work[32 * i:32 * i + 32, 32 * j:32 * j + 32] = block

    for o in range(8):
        chip, core = o // 2, o % 2
        left = (chip + 3) % 4 * 2 + core
        right = (chip + 1) % 4 * 2 + (core + chip // 2) % 2
        pair = chip * 2 + (core + 1 + chip // 2) % 2
        top = jnp.concatenate([gram_a_ref[o], gram_b_ref[o, 0:8]], axis=0)
        fold = gram_b_ref[o, 8:16]
        place(o, o, top[:, :32])
        place(o, o ^ 1, top[:, 32:64])
        place(o, left, top[:, 64:96])
        place(right, pair, top[:, 96:])
        place(right, left, jnp.concatenate([fold[:, 32 * q:32 * q + 32] for q in range(4)], axis=0))
    eye = (lax.broadcasted_iota(jnp.int32, (SIZE, SIZE), 0) == lax.broadcasted_iota(jnp.int32, (SIZE, SIZE), 1)).astype(F32)
    upper = lax.broadcasted_iota(jnp.int32, (SIZE, SIZE), 0) <= lax.broadcasted_iota(jnp.int32, (SIZE, SIZE), 1)
    lower = lax.broadcasted_iota(jnp.int32, (SIZE, SIZE), 0) >= lax.broadcasted_iota(jnp.int32, (SIZE, SIZE), 1)
    block = work[:SIZE, :SIZE]
    later = None
    for p in range(256 // SIZE):
        a, b = SIZE * p, SIZE * p + SIZE
        if EARLY and later:
            later()
        block = jnp.concatenate([block, eye], axis=1)
        solved = factor_block([block[8 * s:8 * s + 8] for s in range(SIZE // 8)])
        if later and not EARLY:
            later()
        own = jnp.where(lower, solved[:, SIZE:], 0.0)
        if b < 256:
            c = b + SIZE
            u = exact_dot(own, work[a:b, b:c], NN)
            block = work[b:c, b:c] - exact_dot(u, u, TN)

        def later(a=a, b=b, own=own, solved=solved, u=u):
            factor_ref[a:b, a:b] = jnp.where(upper, solved[:, :SIZE], 0.0)
            inv[a:b, a:b] = own
            if a > 0:
                inv[a:b, :a] = exact_dot(own, rest[a:b, :a], NN)
            if b < 256:
                c = b + SIZE
                factor_ref[a:b, b:c] = u
                whole = u
                if c < 256:
                    v = exact_dot(own, work[a:b, c:], NN)
                    factor_ref[a:b, c:] = v
                    whole = jnp.concatenate([u, v], axis=1)
                    work[b:c, c:] = work[b:c, c:] - exact_dot(u, v, TN)
                    work[c:, c:] = work[c:, c:] - exact_dot(v, v, TN)
                rest[b:, :b] = rest[b:, :b] - exact_dot(whole, inv[a:b, :b], TN)

    later()
    orb = lax.axis_index("orb")
    mine = inv[pl.ds(pl.multiple_of(orb * 32, 32), 32), :]
    high = mine.astype(BF16)
    left = mine - high.astype(F32)
    mid = left.astype(BF16)
    tail = (left - mid.astype(F32)).astype(BF16)
    stack = jnp.concatenate([high, mid, tail], axis=0)
    here = pltpu.roll(mine, (256 - orb * 32) % 256, 1)[:, :32].astype(BF16)
    load_f.wait()
    load_l.wait()

    for e in range(8):
        d = lax.dot_general(stack, filt[e].reshape(256, 256), NN, preferred_element_type=F32)
        c = lax.dot_general(here, low[e], NN, preferred_element_type=F32)
        basis_ref[:, e * 256:(e + 1) * 256] = d[:32] + (d[32:64] + (d[64:] + c))


def finish_call(gram_a, gram_b, filt, low):
    outside = pl.BlockSpec(memory_space=pltpu.HBM)
    vmem = pl.BlockSpec(memory_space=pltpu.VMEM)
    return pl.pallas_call(
        finish_kernel,
        out_shape=(jax.ShapeDtypeStruct((32, 2048), F32), jax.ShapeDtypeStruct((256, 256), F32)),
        in_specs=[outside] * 4,
        out_specs=(vmem, vmem),
        scratch_shapes=[
            *[pltpu.VMEM((256, 256), F32)] * 3,
            pltpu.VMEM((8, 24, 128), F32), pltpu.VMEM((8, 16, 128), F32),
            pltpu.VMEM((8, 8, 32, 256), BF16), pltpu.VMEM((8, 32, 256), BF16), DMA((4,)),
        ],
        compiler_params=pltpu.CompilerParams(vmem_limit_bytes=67043328),
        name="finish",
    )(gram_a, gram_b, filt, low)


def shards(hamiltonian, orbitals, adjacency):
    return finish_call(*filter_call(hamiltonian, orbitals, adjacency))


def solution(mesh):
    in_specs = (P("space", None, None, None), P("orb", "space"), P("space", None))
    out_specs = (P("orb", "space"), P())
    return jax.shard_map(shards, mesh=mesh, in_specs=in_specs, out_specs=out_specs, check_vma=False)
```

```python
import functools

import jax
import jax.numpy as jnp
from jax import lax
from jax.experimental import pallas as pl
from jax.experimental.pallas import tpu as pltpu
from jax.sharding import PartitionSpec as P

MESH = pl.DeviceIdType.MESH
CENTRE = 0.25
RADIUS = 0.75
F32, BF16 = jnp.float32, jnp.bfloat16
NT = (((1,), (1,)), ((), ()))
DMA = pltpu.SemaphoreType.DMA


def remote(src, dst, send, recv, **where):
    return pltpu.make_async_remote_copy(
        src_ref=src, dst_ref=dst, send_sem=send, recv_sem=recv, device_id=where, device_id_type=MESH
    )


def loop(n, body):
    lax.fori_loop(0, n, lambda i, c: (body(i), c)[1], 0)


def filter_kernel(
    ham_hbm, orb_hbm, adj_hbm, gram_a_out, gram_b_out, filt_out, low_out,
    ham, adj, lev0, lev1, lev2, lo0, hi0, lo1, hi1, lo2, hi2, part, low, filt, near_sum, far_sum,
    za, ya, yb, zb, gram_a, gram_b,
    ham_sem, in_sem, token, halo_send, halo_recv, ag_send, ag_recv, gg_send, gg_recv,
    red_send, red_recv, out_sem,
):
    level, halo = (lev0, lev1, lev2), ((lo0, hi0), (lo1, hi1), (lo2, hi2))
    space, orb = lax.axis_index("space"), lax.axis_index("orb")
    y, z = space // 8, space % 8
    chip, core = orb // 2, orb % 2
    after, before = (space + 1) % 64, (space + 63) % 64
    chip_r, chip_l, chip_x = (chip + 1) % 4, (chip + 3) % 4, (chip + 2) % 4
    partner = chip * 2 + 1 - core
    right, left = chip_r * 2 + core, chip_l * 2 + core
    left_to = chip_l * 2 + (core + chip_l // 2) % 2
    from_l = left
    from_r = chip_r * 2 + (core + chip // 2) % 2
    from_x = chip_x * 2 + core
    from_y = chip_x * 2 + (core + chip_r // 2) % 2
    pair = chip * 2 + (core + 1 + chip // 2) % 2

    def load_ham(e):
        return pltpu.make_async_copy(ham_hbm.at[e], ham.at[e], ham_sem.at[e])

    def load_level(e):
        src = orb_hbm.at[:, pl.ds(pl.multiple_of(e * 256, 256), 256)]
        return pltpu.make_async_copy(src, lev0.at[e], in_sem.at[e])

    load_adj = pltpu.make_async_copy(adj_hbm, adj, in_sem.at[8])

    close = (
        {"space": after}, {"space": before},
        {"space": y * 8 + (z + 1) % 8}, {"space": y * 8 + (z + 7) % 8},
        {"space": (y + 1) % 8 * 8 + z}, {"space": (y + 7) % 8 * 8 + z},
        {"orb": partner}, {"orb": chip_r * 2}, {"orb": chip_r * 2 + 1}, {"orb": chip_l * 2}, {"orb": chip_l * 2 + 1},
    )
    bar = pltpu.get_barrier_semaphore()
    for where in close:
        pl.semaphore_signal(bar, inc=1, device_id=where, device_id_type=MESH)
    load_adj.start()
    loop(8, lambda e: load_level(e).start())
    loop(8, lambda e: load_ham(e).start())
    pl.semaphore_wait(bar, len(close))

    def halo_copy(n, side, e):
        src = orb_hbm.at[:, pl.ds(pl.multiple_of(e * 256, 256), 256)] if n == 0 else level[n].at[e]
        return remote(src, halo[n][side].at[e], halo_send.at[n, side, e], halo_recv.at[n, side, e],
                      space=after if side == 0 else before)

    def start0(e):
        halo_copy(0, 0, e).start()
        halo_copy(0, 1, e).start()

    loop(8, start0)

    def pass_token(n):
        for where in close:
            pl.semaphore_signal(token.at[n], inc=1, device_id=where, device_id_type=MESH)

    def take_token(n):
        pl.semaphore_wait(token.at[n], len(close))

    pass_token(0)

    def gather(kind, t):
        who = (orb, orb, orb, from_l, from_r, from_x, from_l, from_r, from_y)[kind]
        dst = (right, left_to, partner, partner, partner, partner, right, left, partner)[kind]
        send = (0, 1, 2, 3, 4, 5, 6, 6, 5)[kind]
        slot = (0, 1, 2, 3, 4, 5, 6, 6, 5)[kind]
        return remote(filt.at[t, who], filt.at[t, who], ag_send.at[send, t], ag_recv.at[slot, t], orb=dst)

    def arrived(slot, t):
        remote(filt.at[t, orb], filt.at[t, orb], ag_send.at[0, t], ag_recv.at[slot, t], orb=partner).wait_recv()

    def dot(v, h):
        return lax.dot_general(v, h, NT, preferred_element_type=F32)

    load_adj.wait()
    loop(8, lambda e: load_level(e).wait())
    for n in range(3):
        def inner(e, n=n):
            if n == 0:
                load_ham(e).wait()
            total = dot(level[n][e], ham[e, 0])
            for f in range(2, 6):
                total = total + dot(level[n][adj[e, f] & 7], ham[e, f + 1])
            part[e] = total

        loop(8, inner)
        take_token(n)
        if n < 2:
            pass_token(n + 1)

        def landed(e, n=n):
            halo_copy(n, 0, e).wait_recv()
            halo_copy(n, 1, e).wait_recv()

        loop(8, landed)

        def outer(group, n=n):
            ids = [group * 4 + i for i in range(4)]
            totals = []
            for e in ids:
                total = part[e] + dot(halo[n][0][adj[e, 0] & 7], ham[e, 1])
                total = total + dot(halo[n][1][adj[e, 1] & 7], ham[e, 2])
                total = (total - CENTRE * level[n][e].astype(F32)) * (1.0 / RADIUS)
                if n > 0:
                    total = 2.0 * total - level[n - 1][e].astype(F32)
                totals.append(total)
            for e, total in zip(ids, totals):
                if n < 2:
                    level[n + 1][e] = total.astype(BF16)
                else:
                    high = total.astype(BF16)
                    filt[e, orb] = high
                    low[e] = (total - high.astype(F32)).astype(BF16)
            for e in ids:
                if n < 2:
                    halo_copy(n + 1, 0, e).start()
                    halo_copy(n + 1, 1, e).start()
                else:
                    for kind in range(3):
                        gather(kind, e).start()

        loop(2, outer)

    near_sum[...] = jnp.zeros_like(near_sum)
    far_sum[...] = jnp.zeros_like(far_sum)

    def product(half):
        mine, mate, west, east, twin = [], [], [], [], []
        for t in [half * 2 + i for i in range(2)]:
            for slot in range(3):
                arrived(slot, t)
            mine.append(filt[t, orb])
            mate.append(filt[t, partner])
            west.append(filt[t, from_l])
            east.append(filt[t, from_r])
            twin.append(filt[t, pair])
        mine, mate, west, east, twin = (jnp.concatenate(x, axis=1) for x in (mine, mate, west, east, twin))
        near_sum[...] += dot(mine, jnp.concatenate([mine, mate, west, mine], axis=0))
        far_sum[...] += dot(east, jnp.concatenate([west, west, west, twin], axis=0))

    loop(4, product)

    order = (4, 3, 5, 2, 6, 1, 7)
    bufs = ((za, ya), (yb, zb))

    def red(stage, half, d):
        along_z = stage == half
        buf = bufs[half][stage]
        mine = z if along_z else y
        where = y * 8 + (z + d) % 8 if along_z else ((y + d) % 8) * 8 + z
        return remote(buf.at[mine], buf.at[mine],
                      red_send.at[stage, half, d], red_recv.at[stage, half, d], space=where)

    def summed(stage, half):
        buf = bufs[half][stage]
        for d in order:
            red(stage, half, d).wait_recv()
        total = buf[0]
        for i in range(1, 8):
            total = total + buf[i]
        return total

    lane = lax.broadcasted_iota(jnp.int32, (32, 128), 1)
    main = jnp.where(lane < 96, near_sum[...], far_sum[...])
    lane8 = lax.broadcasted_iota(jnp.int32, (8, 128), 1)
    fold = far_sum[0:8]
    fold = jnp.where(lane8 < 32, fold, far_sum[8:16])
    fold = jnp.where(lane8 < 64, fold, far_sum[16:24])
    rest = jnp.where(lane8 < 96, fold, pltpu.roll(far_sum[24:32], 96, 1))
    za[z] = main[:24]
    yb[y, 0:8] = main[24:]
    yb[y, 8:16] = rest
    for half in range(2):
        for d in order:
            red(0, half, d).start()

    def pass_on(t):
        gather(6, t).start()
        gather(7, t + 4).start()

    def relay(t):
        gather(3, t).start()
        gather(4, t).start()

    loop(4, pass_on)
    loop(8, relay)
    for half in range(2):
        total = summed(0, half)
        if half == 0:
            ya[y] = total
        else:
            zb[z] = total
        for d in order:
            red(1, half, d).start()

    def across_first(t):
        arrived(6, t)
        gather(5, t).start()

    def across_second(t):
        arrived(6, t + 4)
        gather(8, t + 4).start()

    loop(4, across_first)
    loop(4, across_second)

    def share(half, d):
        buf = gram_b if half else gram_a
        return remote(buf.at[orb], buf.at[orb], gg_send.at[half, d], gg_recv.at[half, d], orb=(orb + d) % 8)

    for half in range(2):
        total = summed(1, half)
        (gram_b if half else gram_a)[orb] = total
        for d in order:
            share(half, d).start()

    def rest_landed(t):
        for slot in (3, 4, 5):
            arrived(slot, t)

    loop(8, rest_landed)
    out_f = pltpu.make_async_copy(filt, filt_out, out_sem.at[0])
    out_f.start()
    out_l = pltpu.make_async_copy(low, low_out, out_sem.at[1])
    out_l.start()
    for n in range(3):
        def sent(e, n=n):
            halo_copy(n, 0, e).wait_send()
            halo_copy(n, 1, e).wait_send()
        loop(8, sent)

    def gathered(t):
        for kind in range(7):
            gather(kind, t).wait_send()

    loop(8, gathered)
    for stage in range(2):
        for half in range(2):
            for d in order:
                red(stage, half, d).wait_send()
    for half in range(2):
        for d in order:
            share(half, d).wait_recv()
    out_a = pltpu.make_async_copy(gram_a, gram_a_out, out_sem.at[2])
    out_a.start()
    out_b = pltpu.make_async_copy(gram_b, gram_b_out, out_sem.at[3])
    out_b.start()
    for half in range(2):
        for d in order:
            share(half, d).wait_send()
    for out in (out_f, out_l, out_a, out_b):
        out.wait()


def filter_call(hamiltonian, orbitals, adjacency):
    anywhere = pl.BlockSpec(memory_space=pl.ANY)
    outside = pl.BlockSpec(memory_space=pltpu.HBM)
    return pl.pallas_call(
        filter_kernel,
        out_shape=(
            jax.ShapeDtypeStruct((8, 24, 128), F32),
            jax.ShapeDtypeStruct((8, 16, 128), F32),
            jax.ShapeDtypeStruct((8, 8, 32, 256), BF16),
            jax.ShapeDtypeStruct((8, 32, 256), BF16),
        ),
        in_specs=[outside, outside, outside],
        out_specs=(anywhere,) * 4,
        scratch_shapes=[
            pltpu.VMEM((8, 7, 256, 256), BF16),
            pltpu.SMEM((8, 6), jnp.int32),
            *[pltpu.VMEM((8, 32, 256), BF16)] * 9,
            pltpu.VMEM((8, 32, 256), F32),
            pltpu.VMEM((8, 32, 256), BF16),
            pltpu.VMEM((8, 8, 32, 256), BF16),
            pltpu.VMEM((32, 128), F32), pltpu.VMEM((32, 128), F32),
            *[pltpu.VMEM((8, 24, 128), F32)] * 2,
            *[pltpu.VMEM((8, 16, 128), F32)] * 2,
            pltpu.VMEM((8, 24, 128), F32), pltpu.VMEM((8, 16, 128), F32),
            DMA((8,)), DMA((9,)), pltpu.SemaphoreType.REGULAR((3,)),
            DMA((3, 2, 8)), DMA((3, 2, 8)),
            DMA((7, 8)), DMA((7, 8)),
            DMA((2, 8)), DMA((2, 8)),
            DMA((2, 2, 8)), DMA((2, 2, 8)),
            DMA((4,)),
        ],
        compiler_params=pltpu.CompilerParams(
            collective_id=0, has_side_effects=True, vmem_limit_bytes=67043328
        ),
        name="filter",
    )(hamiltonian, orbitals, adjacency)


SIZE = 64
EARLY = False
TN = (((0,), (0,)), ((), ()))
NN = (((1,), (0,)), ((), ()))


def exact_dot(a, b, dims):
    return lax.dot_general(a, b, dims, precision=lax.Precision.HIGHEST, preferred_element_type=F32)


def spread(x, i, j):
    return jnp.broadcast_to(x[i:i + 1, j:j + 1], (8, 128))


def lane_spread(x, j):
    return jnp.take_along_axis(x[:, :128], jnp.full((8, 128), j, jnp.int32), axis=1)


def factor_block(tiles):
    n, width = len(tiles), tiles[0].shape[1]
    sub = lax.broadcasted_iota(jnp.int32, (8, width), 0)
    tiles = list(tiles)
    done = []
    for s in range(n):
        tile = tiles[s]
        own = [lane_spread(tile, 8 * s + j) for j in range(8)]
        at = [[jnp.broadcast_to(own[j][i:i + 1, :], (8, 128)) if j >= i else None for j in range(8)] for i in range(8)]
        rows = [jnp.broadcast_to(tile[k:k + 1, :], (8, width)) for k in range(8)]
        cols = {g: [lane_spread(tiles[g], 8 * s + k) for k in range(8)]
                for g in range(s + 1, n)}
        wide = lambda x: jnp.concatenate([x] * (width // 128), axis=1)
        for k in range(8):
            r = lax.rsqrt(at[k][k])
            rows[k] = rows[k] * wide(r)
            for j in range(k + 1, 8):
                at[k][j] = at[k][j] * r
            for g in cols:
                cols[g][k] = cols[g][k] * r
            for i in range(k + 1, 8):
                for j in range(i, 8):
                    at[i][j] = at[i][j] - at[k][i] * at[k][j]
                rows[i] = rows[i] - wide(at[k][i]) * rows[k]
                for g in cols:
                    cols[g][i] = cols[g][i] - at[k][i] * cols[g][k]
        for g in cols:
            t = tiles[g]
            for k in range(8):
                t = t - wide(cols[g][k]) * rows[k]
            tiles[g] = t
        out = rows[0]
        for k in range(1, 8):
            out = jnp.where(sub == k, rows[k], out)
        done.append(out)
    return jnp.concatenate(done, axis=0)


def finish_kernel(
    gram_a_hbm, gram_b_hbm, filt_hbm, low_hbm, basis_ref, factor_ref,
    work, rest, inv, gram_a_ref, gram_b_ref, filt, low, sem,
):
    load_a = pltpu.make_async_copy(gram_a_hbm, gram_a_ref, sem.at[2])
    load_a.start()
    load_b = pltpu.make_async_copy(gram_b_hbm, gram_b_ref, sem.at[3])
    load_b.start()
    load_f = pltpu.make_async_copy(filt_hbm, filt, sem.at[0])
    load_f.start()
    load_l = pltpu.make_async_copy(low_hbm, low, sem.at[1])
    load_l.start()
    rest[...] = jnp.zeros_like(rest)
    inv[...] = jnp.zeros_like(inv)
    factor_ref[...] = jnp.zeros_like(factor_ref)
    load_a.wait()
    load_b.wait()

    def place(i, j, block):
        if 32 * i // SIZE > 32 * j // SIZE:
            i, j, block = j, i, block.T
        work[32 * i:32 * i + 32, 32 * j:32 * j + 32] = block

    for o in range(8):
        chip, core = o // 2, o % 2
        left = (chip + 3) % 4 * 2 + core
        right = (chip + 1) % 4 * 2 + (core + chip // 2) % 2
        pair = chip * 2 + (core + 1 + chip // 2) % 2
        top = jnp.concatenate([gram_a_ref[o], gram_b_ref[o, 0:8]], axis=0)
        fold = gram_b_ref[o, 8:16]
        place(o, o, top[:, :32])
        place(o, o ^ 1, top[:, 32:64])
        place(o, left, top[:, 64:96])
        place(right, pair, top[:, 96:])
        place(right, left, jnp.concatenate([fold[:, 32 * q:32 * q + 32] for q in range(4)], axis=0))
    eye = (lax.broadcasted_iota(jnp.int32, (SIZE, SIZE), 0) == lax.broadcasted_iota(jnp.int32, (SIZE, SIZE), 1)).astype(F32)
    upper = lax.broadcasted_iota(jnp.int32, (SIZE, SIZE), 0) <= lax.broadcasted_iota(jnp.int32, (SIZE, SIZE), 1)
    lower = lax.broadcasted_iota(jnp.int32, (SIZE, SIZE), 0) >= lax.broadcasted_iota(jnp.int32, (SIZE, SIZE), 1)
    block = work[:SIZE, :SIZE]
    later = None
    for p in range(256 // SIZE):
        a, b = SIZE * p, SIZE * p + SIZE
        if EARLY and later:
            later()
        block = jnp.concatenate([block, eye], axis=1)
        solved = factor_block([block[8 * s:8 * s + 8] for s in range(SIZE // 8)])
        if later and not EARLY:
            later()
        own = jnp.where(lower, solved[:, SIZE:], 0.0)
        if b < 256:
            c = b + SIZE
            u = exact_dot(own, work[a:b, b:c], NN)
            block = work[b:c, b:c] - exact_dot(u, u, TN)

        def later(a=a, b=b, own=own, solved=solved, u=u):
            factor_ref[a:b, a:b] = jnp.where(upper, solved[:, :SIZE], 0.0)
            inv[a:b, a:b] = own
            if a > 0:
                inv[a:b, :a] = exact_dot(own, rest[a:b, :a], NN)
            if b < 256:
                c = b + SIZE
                factor_ref[a:b, b:c] = u
                whole = u
                if c < 256:
                    v = exact_dot(own, work[a:b, c:], NN)
                    factor_ref[a:b, c:] = v
                    whole = jnp.concatenate([u, v], axis=1)
                    work[b:c, c:] = work[b:c, c:] - exact_dot(u, v, TN)
                    work[c:, c:] = work[c:, c:] - exact_dot(v, v, TN)
                rest[b:, :b] = rest[b:, :b] - exact_dot(whole, inv[a:b, :b], TN)

    later()
    orb = lax.axis_index("orb")
    mine = inv[pl.ds(pl.multiple_of(orb * 32, 32), 32), :]
    high = mine.astype(BF16)
    left = mine - high.astype(F32)
    mid = left.astype(BF16)
    tail = (left - mid.astype(F32)).astype(BF16)
    stack = jnp.concatenate([high, mid, tail], axis=0)
    here = pltpu.roll(mine, (256 - orb * 32) % 256, 1)[:, :32].astype(BF16)
    load_f.wait()
    load_l.wait()

    for e in range(8):
        d = lax.dot_general(stack, filt[e].reshape(256, 256), NN, preferred_element_type=F32)
        c = lax.dot_general(here, low[e], NN, preferred_element_type=F32)
        basis_ref[:, e * 256:(e + 1) * 256] = d[:32] + (d[32:64] + (d[64:] + c))


def finish_call(gram_a, gram_b, filt, low):
    outside = pl.BlockSpec(memory_space=pltpu.HBM)
    vmem = pl.BlockSpec(memory_space=pltpu.VMEM)
    return pl.pallas_call(
        finish_kernel,
        out_shape=(jax.ShapeDtypeStruct((32, 2048), F32), jax.ShapeDtypeStruct((256, 256), F32)),
        in_specs=[outside] * 4,
        out_specs=(vmem, vmem),
        scratch_shapes=[
            *[pltpu.VMEM((256, 256), F32)] * 3,
            pltpu.VMEM((8, 24, 128), F32), pltpu.VMEM((8, 16, 128), F32),
            pltpu.VMEM((8, 8, 32, 256), BF16), pltpu.VMEM((8, 32, 256), BF16), DMA((4,)),
        ],
        compiler_params=pltpu.CompilerParams(vmem_limit_bytes=67043328),
        name="finish",
    )(gram_a, gram_b, filt, low)


def shards(hamiltonian, orbitals, adjacency):
    return finish_call(*filter_call(hamiltonian, orbitals, adjacency))


def solution(mesh):
    in_specs = (P("space", None, None, None), P("orb", "space"), P("space", None))
    out_specs = (P("orb", "space"), P())
    return jax.shard_map(shards, mesh=mesh, in_specs=in_specs, out_specs=out_specs, check_vma=False)
```

```python
import functools

import jax
import jax.numpy as jnp
from jax import lax
from jax.experimental import pallas as pl
from jax.experimental.pallas import tpu as pltpu
from jax.sharding import PartitionSpec as P

MESH = pl.DeviceIdType.MESH
CENTRE = 0.25
RADIUS = 0.75
F32, BF16 = jnp.float32, jnp.bfloat16
NT = (((1,), (1,)), ((), ()))
DMA = pltpu.SemaphoreType.DMA


def remote(src, dst, send, recv, **where):
    return pltpu.make_async_remote_copy(
        src_ref=src, dst_ref=dst, send_sem=send, recv_sem=recv, device_id=where, device_id_type=MESH
    )


def loop(n, body):
    lax.fori_loop(0, n, lambda i, c: (body(i), c)[1], 0)


def filter_kernel(
    ham_hbm, orb_hbm, adj_hbm, gram_a_out, gram_b_out, filt_out, low_out,
    ham, adj, lev0, lev1, lev2, lo0, hi0, lo1, hi1, lo2, hi2, part, low, filt, near_sum, far_sum,
    za, ya, yb, zb, gram_a, gram_b,
    ham_sem, in_sem, token, halo_send, halo_recv, ag_send, ag_recv, gg_send, gg_recv,
    red_send, red_recv, out_sem,
):
    level, halo = (lev0, lev1, lev2), ((lo0, hi0), (lo1, hi1), (lo2, hi2))
    space, orb = lax.axis_index("space"), lax.axis_index("orb")
    y, z = space // 8, space % 8
    chip, core = orb // 2, orb % 2
    after, before = (space + 1) % 64, (space + 63) % 64
    chip_r, chip_l, chip_x = (chip + 1) % 4, (chip + 3) % 4, (chip + 2) % 4
    partner = chip * 2 + 1 - core
    right, left = chip_r * 2 + core, chip_l * 2 + core
    left_to = chip_l * 2 + (core + chip_l // 2) % 2
    from_l = left
    from_r = chip_r * 2 + (core + chip // 2) % 2
    from_x = chip_x * 2 + core
    from_y = chip_x * 2 + (core + chip_r // 2) % 2
    pair = chip * 2 + (core + 1 + chip // 2) % 2

    def load_ham(e):
        return pltpu.make_async_copy(ham_hbm.at[e], ham.at[e], ham_sem.at[e])

    def load_level(e):
        src = orb_hbm.at[:, pl.ds(pl.multiple_of(e * 256, 256), 256)]
        return pltpu.make_async_copy(src, lev0.at[e], in_sem.at[e])

    load_adj = pltpu.make_async_copy(adj_hbm, adj, in_sem.at[8])

    close = (
        {"space": after}, {"space": before},
        {"space": y * 8 + (z + 1) % 8}, {"space": y * 8 + (z + 7) % 8},
        {"space": (y + 1) % 8 * 8 + z}, {"space": (y + 7) % 8 * 8 + z},
        {"orb": partner}, {"orb": chip_r * 2}, {"orb": chip_r * 2 + 1}, {"orb": chip_l * 2}, {"orb": chip_l * 2 + 1},
    )
    bar = pltpu.get_barrier_semaphore()
    for where in close:
        pl.semaphore_signal(bar, inc=1, device_id=where, device_id_type=MESH)
    load_adj.start()
    loop(8, lambda e: load_level(e).start())
    loop(8, lambda e: load_ham(e).start())
    pl.semaphore_wait(bar, len(close))

    def halo_copy(n, side, e):
        src = orb_hbm.at[:, pl.ds(pl.multiple_of(e * 256, 256), 256)] if n == 0 else level[n].at[e]
        return remote(src, halo[n][side].at[e], halo_send.at[n, side, e], halo_recv.at[n, side, e],
                      space=after if side == 0 else before)

    def start0(e):
        halo_copy(0, 0, e).start()
        halo_copy(0, 1, e).start()

    loop(8, start0)

    def pass_token(n):
        for where in close:
            pl.semaphore_signal(token.at[n], inc=1, device_id=where, device_id_type=MESH)

    def take_token(n):
        pl.semaphore_wait(token.at[n], len(close))

    pass_token(0)

    def gather(kind, t):
        who = (orb, orb, orb, from_l, from_r, from_x, from_l, from_r, from_y)[kind]
        dst = (right, left_to, partner, partner, partner, partner, right, left, partner)[kind]
        send = (0, 1, 2, 3, 4, 5, 6, 6, 5)[kind]
        slot = (0, 1, 2, 3, 4, 5, 6, 6, 5)[kind]
        return remote(filt.at[t, who], filt.at[t, who], ag_send.at[send, t], ag_recv.at[slot, t], orb=dst)

    def arrived(slot, t):
        remote(filt.at[t, orb], filt.at[t, orb], ag_send.at[0, t], ag_recv.at[slot, t], orb=partner).wait_recv()

    def dot(v, h):
        return lax.dot_general(v, h, NT, preferred_element_type=F32)

    load_adj.wait()
    loop(8, lambda e: load_level(e).wait())
    for n in range(3):
        def inner(e, n=n):
            if n == 0:
                load_ham(e).wait()
            total = dot(level[n][e], ham[e, 0])
            for f in range(2, 6):
                total = total + dot(level[n][adj[e, f] & 7], ham[e, f + 1])
            part[e] = total

        loop(8, inner)
        take_token(n)
        if n < 2:
            pass_token(n + 1)

        def landed(e, n=n):
            halo_copy(n, 0, e).wait_recv()
            halo_copy(n, 1, e).wait_recv()

        loop(8, landed)

        def outer(group, n=n):
            ids = [group * 4 + i for i in range(4)]
            totals = []
            for e in ids:
                total = part[e] + dot(halo[n][0][adj[e, 0] & 7], ham[e, 1])
                total = total + dot(halo[n][1][adj[e, 1] & 7], ham[e, 2])
                total = (total - CENTRE * level[n][e].astype(F32)) * (1.0 / RADIUS)
                if n > 0:
                    total = 2.0 * total - level[n - 1][e].astype(F32)
                totals.append(total)
            for e, total in zip(ids, totals):
                if n < 2:
                    level[n + 1][e] = total.astype(BF16)
                else:
                    high = total.astype(BF16)
                    filt[e, orb] = high
                    low[e] = (total - high.astype(F32)).astype(BF16)
            for e in ids:
                if n < 2:
                    halo_copy(n + 1, 0, e).start()
                    halo_copy(n + 1, 1, e).start()
                else:
                    for kind in range(3):
                        gather(kind, e).start()

        loop(2, outer)

    near_sum[...] = jnp.zeros_like(near_sum)
    far_sum[...] = jnp.zeros_like(far_sum)

    def product(half):
        mine, mate, west, east, twin = [], [], [], [], []
        for t in [half * 2 + i for i in range(2)]:
            for slot in range(3):
                arrived(slot, t)
            mine.append(filt[t, orb])
            mate.append(filt[t, partner])
            west.append(filt[t, from_l])
            east.append(filt[t, from_r])
            twin.append(filt[t, pair])
        mine, mate, west, east, twin = (jnp.concatenate(x, axis=1) for x in (mine, mate, west, east, twin))
        near_sum[...] += dot(mine, jnp.concatenate([mine, mate, west, mine], axis=0))
        far_sum[...] += dot(east, jnp.concatenate([west, west, west, twin], axis=0))

    loop(4, product)

    order = (4, 3, 5, 2, 6, 1, 7)
    bufs = ((za, ya), (yb, zb))

    def red(stage, half, d):
        along_z = stage == half
        buf = bufs[half][stage]
        mine = z if along_z else y
        where = y * 8 + (z + d) % 8 if along_z else ((y + d) % 8) * 8 + z
        return remote(buf.at[mine], buf.at[mine],
                      red_send.at[stage, half, d], red_recv.at[stage, half, d], space=where)

    def summed(stage, half):
        buf = bufs[half][stage]
        for d in order:
            red(stage, half, d).wait_recv()
        total = buf[0]
        for i in range(1, 8):
            total = total + buf[i]
        return total

    lane = lax.broadcasted_iota(jnp.int32, (32, 128), 1)
    main = jnp.where(lane < 96, near_sum[...], far_sum[...])
    lane8 = lax.broadcasted_iota(jnp.int32, (8, 128), 1)
    fold = far_sum[0:8]
    fold = jnp.where(lane8 < 32, fold, far_sum[8:16])
    fold = jnp.where(lane8 < 64, fold, far_sum[16:24])
    rest = jnp.where(lane8 < 96, fold, pltpu.roll(far_sum[24:32], 96, 1))
    za[z] = main[:24]
    yb[y, 0:8] = main[24:]
    yb[y, 8:16] = rest
    for half in range(2):
        for d in order:
            red(0, half, d).start()

    def pass_on(t):
        gather(6, t).start()
        gather(7, t + 4).start()

    def relay(t):
        gather(3, t).start()
        gather(4, t).start()

    loop(4, pass_on)
    loop(8, relay)
    for half in range(2):
        total = summed(0, half)
        if half == 0:
            ya[y] = total
        else:
            zb[z] = total
        for d in order:
            red(1, half, d).start()

    def across_first(t):
        arrived(6, t)
        gather(5, t).start()

    def across_second(t):
        arrived(6, t + 4)
        gather(8, t + 4).start()

    loop(4, across_first)
    loop(4, across_second)

    def share(half, d):
        buf = gram_b if half else gram_a
        return remote(buf.at[orb], buf.at[orb], gg_send.at[half, d], gg_recv.at[half, d], orb=(orb + d) % 8)

    for half in range(2):
        total = summed(1, half)
        (gram_b if half else gram_a)[orb] = total
        for d in order:
            share(half, d).start()

    def rest_landed(t):
        for slot in (3, 4, 5):
            arrived(slot, t)

    loop(8, rest_landed)
    out_f = pltpu.make_async_copy(filt, filt_out, out_sem.at[0])
    out_f.start()
    out_l = pltpu.make_async_copy(low, low_out, out_sem.at[1])
    out_l.start()
    for n in range(3):
        def sent(e, n=n):
            halo_copy(n, 0, e).wait_send()
            halo_copy(n, 1, e).wait_send()
        loop(8, sent)

    def gathered(t):
        for kind in range(7):
            gather(kind, t).wait_send()

    loop(8, gathered)
    for stage in range(2):
        for half in range(2):
            for d in order:
                red(stage, half, d).wait_send()
    out_a = pltpu.make_async_copy(gram_a, gram_a_out, out_sem.at[2])
    out_b = pltpu.make_async_copy(gram_b, gram_b_out, out_sem.at[3])
    for half, out in enumerate((out_a, out_b)):
        for d in order:
            share(half, d).wait_recv()
        out.start()
    for half in range(2):
        for d in order:
            share(half, d).wait_send()
    for out in (out_f, out_l, out_a, out_b):
        out.wait()


def filter_call(hamiltonian, orbitals, adjacency):
    anywhere = pl.BlockSpec(memory_space=pl.ANY)
    outside = pl.BlockSpec(memory_space=pltpu.HBM)
    return pl.pallas_call(
        filter_kernel,
        out_shape=(
            jax.ShapeDtypeStruct((8, 24, 128), F32),
            jax.ShapeDtypeStruct((8, 16, 128), F32),
            jax.ShapeDtypeStruct((8, 8, 32, 256), BF16),
            jax.ShapeDtypeStruct((8, 32, 256), BF16),
        ),
        in_specs=[outside, outside, outside],
        out_specs=(anywhere,) * 4,
        scratch_shapes=[
            pltpu.VMEM((8, 7, 256, 256), BF16),
            pltpu.SMEM((8, 6), jnp.int32),
            *[pltpu.VMEM((8, 32, 256), BF16)] * 9,
            pltpu.VMEM((8, 32, 256), F32),
            pltpu.VMEM((8, 32, 256), BF16),
            pltpu.VMEM((8, 8, 32, 256), BF16),
            pltpu.VMEM((32, 128), F32), pltpu.VMEM((32, 128), F32),
            *[pltpu.VMEM((8, 24, 128), F32)] * 2,
            *[pltpu.VMEM((8, 16, 128), F32)] * 2,
            pltpu.VMEM((8, 24, 128), F32), pltpu.VMEM((8, 16, 128), F32),
            DMA((8,)), DMA((9,)), pltpu.SemaphoreType.REGULAR((3,)),
            DMA((3, 2, 8)), DMA((3, 2, 8)),
            DMA((7, 8)), DMA((7, 8)),
            DMA((2, 8)), DMA((2, 8)),
            DMA((2, 2, 8)), DMA((2, 2, 8)),
            DMA((4,)),
        ],
        compiler_params=pltpu.CompilerParams(
            collective_id=0, has_side_effects=True, vmem_limit_bytes=67043328
        ),
        name="filter",
    )(hamiltonian, orbitals, adjacency)


SIZE = 64
EARLY = False
TN = (((0,), (0,)), ((), ()))
NN = (((1,), (0,)), ((), ()))


def exact_dot(a, b, dims):
    return lax.dot_general(a, b, dims, precision=lax.Precision.HIGHEST, preferred_element_type=F32)


def spread(x, i, j):
    return jnp.broadcast_to(x[i:i + 1, j:j + 1], (8, 128))


def lane_spread(x, j):
    return jnp.take_along_axis(x[:, :128], jnp.full((8, 128), j, jnp.int32), axis=1)


def factor_block(tiles):
    n, width = len(tiles), tiles[0].shape[1]
    sub = lax.broadcasted_iota(jnp.int32, (8, width), 0)
    tiles = list(tiles)
    done = []
    for s in range(n):
        tile = tiles[s]
        own = [lane_spread(tile, 8 * s + j) for j in range(8)]
        at = [[jnp.broadcast_to(own[j][i:i + 1, :], (8, 128)) if j >= i else None for j in range(8)] for i in range(8)]
        rows = [jnp.broadcast_to(tile[k:k + 1, :], (8, width)) for k in range(8)]
        cols = {g: [lane_spread(tiles[g], 8 * s + k) for k in range(8)]
                for g in range(s + 1, n)}
        wide = lambda x: jnp.concatenate([x] * (width // 128), axis=1)
        for k in range(8):
            r = lax.rsqrt(at[k][k])
            rows[k] = rows[k] * wide(r)
            for j in range(k + 1, 8):
                at[k][j] = at[k][j] * r
            for g in cols:
                cols[g][k] = cols[g][k] * r
            for i in range(k + 1, 8):
                for j in range(i, 8):
                    at[i][j] = at[i][j] - at[k][i] * at[k][j]
                rows[i] = rows[i] - wide(at[k][i]) * rows[k]
                for g in cols:
                    cols[g][i] = cols[g][i] - at[k][i] * cols[g][k]
        for g in cols:
            t = tiles[g]
            for k in range(8):
                t = t - wide(cols[g][k]) * rows[k]
            tiles[g] = t
        out = rows[0]
        for k in range(1, 8):
            out = jnp.where(sub == k, rows[k], out)
        done.append(out)
    return jnp.concatenate(done, axis=0)


def finish_kernel(
    gram_a_hbm, gram_b_hbm, filt_hbm, low_hbm, basis_hbm, factor_hbm,
    basis_ref, factor_ref, work, rest, inv, gram_a_ref, gram_b_ref, filt, low, sem,
):
    load_a = pltpu.make_async_copy(gram_a_hbm, gram_a_ref, sem.at[2])
    load_a.start()
    load_b = pltpu.make_async_copy(gram_b_hbm, gram_b_ref, sem.at[3])
    load_b.start()
    load_f = pltpu.make_async_copy(filt_hbm, filt, sem.at[0])
    load_f.start()
    load_l = pltpu.make_async_copy(low_hbm, low, sem.at[1])
    load_l.start()
    rest[...] = jnp.zeros_like(rest)
    inv[...] = jnp.zeros_like(inv)
    factor_ref[...] = jnp.zeros_like(factor_ref)
    load_a.wait()
    load_b.wait()

    def place(i, j, block):
        if 32 * i // SIZE > 32 * j // SIZE:
            i, j, block = j, i, block.T
        work[32 * i:32 * i + 32, 32 * j:32 * j + 32] = block

    for o in range(8):
        chip, core = o // 2, o % 2
        left = (chip + 3) % 4 * 2 + core
        right = (chip + 1) % 4 * 2 + (core + chip // 2) % 2
        pair = chip * 2 + (core + 1 + chip // 2) % 2
        top = jnp.concatenate([gram_a_ref[o], gram_b_ref[o, 0:8]], axis=0)
        fold = gram_b_ref[o, 8:16]
        place(o, o, top[:, :32])
        place(o, o ^ 1, top[:, 32:64])
        place(o, left, top[:, 64:96])
        place(right, pair, top[:, 96:])
        place(right, left, jnp.concatenate([fold[:, 32 * q:32 * q + 32] for q in range(4)], axis=0))
    eye = (lax.broadcasted_iota(jnp.int32, (SIZE, SIZE), 0) == lax.broadcasted_iota(jnp.int32, (SIZE, SIZE), 1)).astype(F32)
    upper = lax.broadcasted_iota(jnp.int32, (SIZE, SIZE), 0) <= lax.broadcasted_iota(jnp.int32, (SIZE, SIZE), 1)
    lower = lax.broadcasted_iota(jnp.int32, (SIZE, SIZE), 0) >= lax.broadcasted_iota(jnp.int32, (SIZE, SIZE), 1)
    block = work[:SIZE, :SIZE]
    later = None
    for p in range(256 // SIZE):
        a, b = SIZE * p, SIZE * p + SIZE
        if EARLY and later:
            later()
        block = jnp.concatenate([block, eye], axis=1)
        solved = factor_block([block[8 * s:8 * s + 8] for s in range(SIZE // 8)])
        if later and not EARLY:
            later()
        own = jnp.where(lower, solved[:, SIZE:], 0.0)
        if b < 256:
            c = b + SIZE
            u = exact_dot(own, work[a:b, b:c], NN)
            block = work[b:c, b:c] - exact_dot(u, u, TN)

        def later(a=a, b=b, own=own, solved=solved, u=u):
            factor_ref[a:b, a:b] = jnp.where(upper, solved[:, :SIZE], 0.0)
            inv[a:b, a:b] = own
            if a > 0:
                inv[a:b, :a] = exact_dot(own, rest[a:b, :a], NN)
            if b < 256:
                c = b + SIZE
                factor_ref[a:b, b:c] = u
                whole = u
                if c < 256:
                    v = exact_dot(own, work[a:b, c:], NN)
                    factor_ref[a:b, c:] = v
                    whole = jnp.concatenate([u, v], axis=1)
                    work[b:c, c:] = work[b:c, c:] - exact_dot(u, v, TN)
                    work[c:, c:] = work[c:, c:] - exact_dot(v, v, TN)
                rest[b:, :b] = rest[b:, :b] - exact_dot(whole, inv[a:b, :b], TN)

    later()
    store_f = pltpu.make_async_copy(factor_ref, factor_hbm, sem.at[4])
    store_f.start()
    orb = lax.axis_index("orb")
    mine = inv[pl.ds(pl.multiple_of(orb * 32, 32), 32), :]
    high = mine.astype(BF16)
    left = mine - high.astype(F32)
    mid = left.astype(BF16)
    tail = (left - mid.astype(F32)).astype(BF16)
    stack = jnp.concatenate([high, mid, tail], axis=0)
    here = pltpu.roll(mine, (256 - orb * 32) % 256, 1)[:, :32].astype(BF16)
    load_f.wait()
    load_l.wait()

    stores = [store_f]
    for e in range(8):
        d = lax.dot_general(stack, filt[e].reshape(256, 256), NN, preferred_element_type=F32)
        c = lax.dot_general(here, low[e], NN, preferred_element_type=F32)
        basis_ref[:, e * 256:(e + 1) * 256] = d[:32] + (d[32:64] + (d[64:] + c))
        if e % 2:
            part = pl.ds(e * 256 - 256, 512)
            stores.append(pltpu.make_async_copy(basis_ref.at[:, part], basis_hbm.at[:, part], sem.at[5 + e // 2]))
            stores[-1].start()
    for store in stores:
        store.wait()


def finish_call(gram_a, gram_b, filt, low):
    outside = pl.BlockSpec(memory_space=pltpu.HBM)
    return pl.pallas_call(
        finish_kernel,
        out_shape=(jax.ShapeDtypeStruct((32, 2048), F32), jax.ShapeDtypeStruct((256, 256), F32)),
        in_specs=[outside] * 4,
        out_specs=(outside, outside),
        scratch_shapes=[
            pltpu.VMEM((32, 2048), F32), *[pltpu.VMEM((256, 256), F32)] * 4,
            pltpu.VMEM((8, 24, 128), F32), pltpu.VMEM((8, 16, 128), F32),
            pltpu.VMEM((8, 8, 32, 256), BF16), pltpu.VMEM((8, 32, 256), BF16), DMA((9,)),
        ],
        compiler_params=pltpu.CompilerParams(vmem_limit_bytes=67043328),
        name="finish",
    )(gram_a, gram_b, filt, low)


def shards(hamiltonian, orbitals, adjacency):
    return finish_call(*filter_call(hamiltonian, orbitals, adjacency))


def solution(mesh):
    in_specs = (P("space", None, None, None), P("orb", "space"), P("space", None))
    out_specs = (P("orb", "space"), P())
    return jax.shard_map(shards, mesh=mesh, in_specs=in_specs, out_specs=out_specs, check_vma=False)
```
